512 devices in a mesh: occ: 128 (over z_lo, x, y), grp: 4 (over z_hi, core).
Axes of the slice: x: 4, y: 8, z: 8 (z_hi: 2, z_lo: 4; z = z_hi * 4 + z_lo), core: 2. Of those that a mesh axis runs over, the one named last changes fastest.
Arguments:
- slabs: float32 [512, 512, 1024], P(('occ', 'grp')), may hold values from -4 to 4
- occ_energy: float32 [512], replicated, may hold values from -1.5 to -0.3
- vir_energy: float32 [512], replicated, may hold values from 0.1 to 3
- pair_mask: int32 [512, 2], replicated, may hold values from 0 to 1, as said below
Outputs:
- aux_grad: float32 [512, 512, 1024], P(('occ', 'grp'))
- vir_density: float32 [512, 512], P('occ')
The draws below stay inside these ranges and needn't reach their ends.
Inputs may be any that keep to these rules, and one draw needn't show every extreme that they name: Entries are 0 or 1; orbital 0 is paired with all of its 2 partners, and so is every orbital i >= 512 - 1 - 2 (pair_mask[i, k - 1] = 1 for every 1 <= k <= 2 on those rows).
All inputs are finite; a program needn't handle non-finite values.
Results may differ from the reference program's by a relative error of at most 0.0003.
Values sent between devices are 32-bit elements; how exact they have to be, the bound alone decides.
A program may use at most 128 MiB of HBM per device.

```python
import jax
import jax.numpy as jnp
from jax import lax

V = 512
A = 1024
KOFF = 2
NOCC = 512


def draw_pair_mask(key, part):
    ticket = jax.random.randint(jax.random.fold_in(key, 17), (NOCC, KOFF), 0, 5)
    chosen = (ticket < 2).astype(jnp.int32)
    chosen = chosen.at[0].set(1)
    return chosen.at[NOCC - 1 - KOFF:].set(1)


def raised(values, stream_key, source, target, blocks, factor):
    owner, partner = [(jnp.arange(values.shape[position]) // (values.shape[position] // blocks)).reshape([-1 if axis == position else 1 for axis in range(values.ndim)]) for position in (source, target)]
    chosen = jax.random.permutation(stream_key, blocks)[partner]
    strong = (owner == chosen) | (owner == (partner + blocks // 2) % blocks)
    return jnp.where(strong, factor * values, values)


def block_levels(rng, shape, pieces, low, largest):
    loudness = 1.0
    for dim, parts in pieces:
        draws = jax.random.uniform(jax.random.fold_in(jax.random.fold_in(rng, 6), dim), (parts,), jnp.float32, low / len(pieces), largest / len(pieces))
        loudness = loudness * jnp.repeat(jnp.exp(draws), shape[dim] // parts).reshape((-1,) + (1,) * (len(shape) - 1 - dim))
    return loudness


def heavy_noise(own_key, dims, spread, most, split, heavy, kind=jnp.bfloat16):
    entries = spread * jax.random.normal(own_key, dims, jnp.float32)
    if split:
        entries = entries * block_levels(own_key, dims, split, -0.22, 0.18)
    return jnp.clip(raised(entries, jax.random.fold_in(own_key, 3), *heavy), -most, most).astype(kind)


def setup_inputs(seed: int = 0) -> dict:
    streams_of = jax.random.split(jax.random.key(seed), 5)
    return {
        "slabs": heavy_noise(streams_of[0], (NOCC, V, A), 0.15, 4.0, ((0, 512),), (0, 1, 512, 6.0), jnp.float32),
        "occ_energy": jnp.clip(jax.random.uniform(streams_of[1], (NOCC,), jnp.float32, -1.5, -0.3), -1.5, -0.3),
        "vir_energy": jnp.clip(jax.random.uniform(streams_of[2], (V,), jnp.float32, 0.1, 3.0), 0.1, 3.0),
        "pair_mask": draw_pair_mask(jax.random.fold_in(streams_of[4], 71), 0),
    }


highest = lax.Precision.HIGHEST


def pair_terms(left_slab, right_slab, left_energy, right_energy, virtual):
    coulomb = jnp.dot(left_slab, right_slab.T, precision=highest, preferred_element_type=jnp.float32)
    denominator = left_energy + right_energy - virtual[:, None] - virtual[None, :]
    amplitude = coulomb / denominator
    grad_left = jnp.dot(amplitude, right_slab, precision=highest, preferred_element_type=jnp.float32)
    grad_right = jnp.dot(amplitude.T, left_slab, precision=highest, preferred_element_type=jnp.float32)
    density = jnp.dot(amplitude, amplitude.T, precision=highest, preferred_element_type=jnp.float32)
    density = density + jnp.dot(amplitude.T, amplitude, precision=highest, preferred_element_type=jnp.float32)
    return grad_left, grad_right, density


def reference(slabs, occ_energy, vir_energy, pair_mask):
    orbitals = slabs.shape[0]

    def visit(state_pair, orbital):
        grads, density = state_pair
        own_slab = lax.dynamic_index_in_dim(slabs, orbital, 0, keepdims=False)
        own_energy = lax.dynamic_index_in_dim(occ_energy, orbital, 0, keepdims=False)
        grad_left, grad_right, term = pair_terms(own_slab, own_slab, own_energy, own_energy, vir_energy)
        grads = grads.at[orbital].add(grad_left + grad_right)
        density = density + term
        for offset in range(1, KOFF + 1):
            partner = orbital + offset
            clipped = jnp.minimum(partner, orbitals - 1).astype(jnp.int32)
            flag = lax.dynamic_index_in_dim(pair_mask[:, offset - 1], orbital, 0, keepdims=False)
            active = ((flag == 1) & (partner < orbitals)).astype(jnp.float32)
            partner_slab = lax.dynamic_index_in_dim(slabs, clipped, 0, keepdims=False)
            partner_energy = lax.dynamic_index_in_dim(occ_energy, clipped, 0, keepdims=False)
            grad_left, grad_right, term = pair_terms(own_slab, partner_slab, own_energy, partner_energy, vir_energy)
            grads = grads.at[orbital].add(active * grad_left)
            grads = grads.at[clipped].add(active * grad_right)
            density = density + active * term
        return (grads, density), None

    start_state = (jnp.zeros(slabs.shape, jnp.float32), jnp.zeros((slabs.shape[1], slabs.shape[1]), jnp.float32))
    order = jnp.arange(orbitals, dtype=jnp.int32)
    (grads, density), unused = lax.scan(visit, start_state, order)
    return grads, density / orbitals
```

```python
import functools

import jax
import jax.numpy as jnp
from jax import lax
from jax.experimental import pallas as pl
from jax.experimental.pallas import tpu as pltpu
from jax.sharding import PartitionSpec as P

MESH = pl.DeviceIdType.MESH
V, A, N = 512, 1024, 512
BLOCK = 128
PIECE = 32
PIECES = V // PIECE
PER_BLOCK = BLOCK // PIECE
bf16, f32 = jnp.bfloat16, jnp.float32


def device(x, y, z, core):
    return (lax.rem(z, 4) * 32 + x * 8 + y, (z // 4) * 2 + core)


def split(value):
    high = value.astype(bf16)
    return high, (value - high.astype(f32)).astype(bf16)


def times(left, right):
    return jnp.dot(left, right, preferred_element_type=f32)


def times_t(left, right):
    return lax.dot_general(left, right, (((1,), (1,)), ((), ())), preferred_element_type=f32)


def kernel(
    slab, occ_ref, vir_ref, mask_ref, grad_out, density_out,
    own_high, own_low, own, other, near, grad, half, vir_col,
    rhs_high, rhs_low, t_high, t_low,
    core_in, x_buf, x_in, y_buf, y_in, z_buf, z_in, last_buf, last_in,
    local_sem, o_send, o_recv, z_send, z_recv, y_send, y_recv, p_send, p_recv,
    c_send, c_recv, xs, xr, ys, yr, zs, zr, ls, lr,
):
    occ, grp = lax.axis_index("occ"), lax.axis_index("grp")
    x, y = lax.rem(occ // 8, 4), lax.rem(occ, 8)
    z_low, z_high, core = occ // 32, grp // 2, lax.rem(grp, 2)
    z = z_high * 4 + z_low
    position = occ * 4 + grp
    partner = device(x, y, z, 1 - core)
    antipode = device(x, y, lax.rem(z + 4, 8), core)
    step = 1 - 2 * z_high
    target, source = occ + step, occ - step
    has_target = (target >= 0) & (target < 128)
    has_source = (source >= 0) & (source < 128)
    gives_z = z_high == core

    load = pltpu.make_async_copy(slab.at[0], own, local_sem.at[0])
    load.start()

    def x_peer(k):
        return device(lax.rem(x + k, 4), y, z, core)

    def y_peer(k):
        return device(x, lax.rem(y + k, 8), z, core)

    def z_peer(k):
        return device(x, y, lax.rem(z + k, 8), core)

    barrier = pltpu.get_barrier_semaphore()
    peers = [partner]
    peers += [x_peer(k) for k in range(1, 4)]
    peers += [y_peer(k) for k in range(1, 8)]
    peers += [z_peer(k) for k in range(1, 8)]
    peers += [(lax.rem(occ + k, 128), grp) for k in (1, 127)]
    for peer in peers:
        pl.semaphore_signal(barrier, inc=1, device_id=peer, device_id_type=MESH)
    pl.semaphore_wait(barrier, len(peers))

    def rows(p):
        return pl.ds(pl.multiple_of(p * PIECE, PIECE), PIECE)

    def spot(kind, p):
        start = ((p // PER_BLOCK) * 3 + kind) * BLOCK + lax.rem(p, PER_BLOCK) * PIECE
        return near.at[pl.ds(pl.multiple_of(start, PIECE), PIECE)]

    def remote(src, dst, send, recv, to):
        return pltpu.make_async_remote_copy(
            src_ref=src, dst_ref=dst, send_sem=send, recv_sem=recv, device_id=to, device_id_type=MESH
        )

    def z_copy(p):
        return remote(slab.at[0, rows(p)], spot(0, p), z_send.at[p], z_recv.at[p], antipode)

    def y_copy(p):
        return remote(spot(0, p), spot(2, p), y_send.at[p], y_recv.at[p], (target, grp))

    def p_copy(p, kind):
        return remote(spot(kind, p), spot(1, p), p_send.at[p], p_recv.at[p], partner)

    o_copy = remote(slab.at[0], other, o_send, o_recv, partner)

    def start_z(p, carry):
        z_copy(p).start()
        return carry

    lax.fori_loop(0, PIECES, start_z, 0)
    o_copy.start()

    load.wait()
    vir_row = vir_ref[...]
    vir_col[...] = jnp.transpose(jnp.broadcast_to(vir_row, (128, V)))
    for m in range(4):
        high, low = split(own[pl.ds(m * 128, 128), :])
        own_high[pl.ds(m * 128, 128), :] = high
        own_low[pl.ds(m * 128, 128), :] = low
    grad[...] = jnp.zeros_like(grad)
    half[...] = jnp.zeros_like(half)

    @pl.when(jnp.logical_not(has_source))
    def _():
        for b in range(4):
            near[pl.ds((3 * b + 2) * BLOCK, BLOCK), :] = jnp.zeros((BLOCK, A), f32)

    @pl.when(jnp.logical_not(has_source) & gives_z)
    def _():
        for b in range(4):
            near[pl.ds((3 * b + 1) * BLOCK, BLOCK), :] = jnp.zeros((BLOCK, A), f32)

    own_energy = occ_ref[position]

    def weight_of(other_index):
        low, high = jnp.minimum(position, other_index), jnp.maximum(position, other_index)
        present = (low >= 0) & (high < N)
        flag = mask_ref[jnp.maximum(low, 0), high - low - 1]
        return jnp.where(present & (flag == 1), 1.0, 0.0).astype(f32)

    def energy_of(other_index):
        return occ_ref[jnp.clip(other_index, 0, N - 1)]

    side = 1 - 2 * core
    o_index, x_index = position + side, position - side
    z_index, y_index = position + 2 * step, position - 2 * step
    facts = {
        "own": (own_energy, jnp.float32(2.0)),
        "o": (energy_of(o_index), weight_of(o_index)),
        "z": (energy_of(z_index), weight_of(z_index)),
        "p": (energy_of(x_index), weight_of(x_index)),
        "y": (energy_of(y_index), weight_of(y_index)),
    }

    def block_terms(pieces):
        width = len(pieces) * BLOCK
        for n, (ref, _, _) in enumerate(pieces):
            high, low = split(ref[...])
            rhs_high[pl.ds(n * BLOCK, BLOCK), :] = high
            rhs_low[pl.ds(n * BLOCK, BLOCK), :] = low
        tiles = []
        for _, number, name in pieces:
            energy, weight = facts[name]
            start = pl.multiple_of(number * BLOCK, BLOCK)
            tiles.append((own_energy + energy - vir_ref[:, pl.ds(start, BLOCK)], weight))

        def rows_of(m, carry):
            band = pl.ds(pl.multiple_of(m * 256, 256), 256)
            left_high, left_low = own_high[band, :], own_low[band, :]
            right_high, right_low = rhs_high[:width, :], rhs_low[:width, :]
            coulomb = times_t(left_high, right_high)
            coulomb += times_t(left_high, right_low)
            coulomb += times_t(left_low, right_high)
            column = vir_col[band, :]
            for n, (base, _) in enumerate(tiles):
                cut = slice(n * BLOCK, (n + 1) * BLOCK)
                high, low = split(coulomb[:, cut] / (base - column))
                t_high[band, cut] = high
                t_low[band, cut] = low
            weighted_high = jnp.concatenate(
                [t_high[band, n * BLOCK:(n + 1) * BLOCK] * tiles[n][1].astype(bf16) for n in range(len(tiles))], axis=1
            )
            weighted_low = jnp.concatenate(
                [t_low[band, n * BLOCK:(n + 1) * BLOCK] * tiles[n][1].astype(bf16) for n in range(len(tiles))], axis=1
            )
            grad[band, :] += (
                times(weighted_high, right_high) + times(weighted_high, right_low) + times(weighted_low, right_high)
            )
            return carry

        lax.fori_loop(0, 2, rows_of, 0)

        def density_rows(m, carry):
            band = pl.ds(pl.multiple_of(m * 256, 256), 256)
            weighted_high = jnp.concatenate(
                [t_high[band, n * BLOCK:(n + 1) * BLOCK] * tiles[n][1].astype(bf16) for n in range(len(tiles))], axis=1
            )
            weighted_low = jnp.concatenate(
                [t_low[band, n * BLOCK:(n + 1) * BLOCK] * tiles[n][1].astype(bf16) for n in range(len(tiles))], axis=1
            )
            for h in range(2):
                other_high = t_high[pl.ds(h * 256, 256), :width]
                other_low = t_low[pl.ds(h * 256, 256), :width]
                half[h, band, :] += (
                    times_t(weighted_high, other_high)
                    + times_t(weighted_high, other_low)
                    + times_t(weighted_low, other_high)
                )
            return carry

        lax.fori_loop(0, 2, density_rows, 0)

    def part(ref, b):
        return ref.at[pl.ds(pl.multiple_of(b * BLOCK, BLOCK), BLOCK)]

    def own_blocks(b, carry):
        block_terms([(part(own, 2 * b), 2 * b, "own"), (part(own, 2 * b + 1), 2 * b + 1, "own")])
        return carry

    lax.fori_loop(0, 2, own_blocks, 0)
    o_copy.wait_recv()

    def other_blocks(b, carry):
        block_terms([(part(other, 2 * b), 2 * b, "o"), (part(other, 2 * b + 1), 2 * b + 1, "o")])
        return carry

    lax.fori_loop(0, 2, other_blocks, 0)

    def take(p, carry):
        z_copy(p).wait_recv()

        @pl.when(has_target)
        def _():
            y_copy(p).start()

        @pl.when(gives_z)
        def _():
            p_copy(p, 0).start()

        return carry

    def pass_on(p, carry):
        @pl.when(has_source)
        def _():
            y_copy(p).wait_recv()

            @pl.when(jnp.logical_not(gives_z))
            def _():
                p_copy(p, 2).start()

        return carry

    def near_blocks(b, carry):
        lax.fori_loop(b * PER_BLOCK, (b + 1) * PER_BLOCK, take, 0)
        lax.fori_loop(b * PER_BLOCK, (b + 1) * PER_BLOCK, pass_on, 0)

        def settle(p, carry):
            @pl.when(has_source | jnp.logical_not(gives_z))
            def _():
                p_copy(p, 0).wait_recv()

            return carry

        lax.fori_loop(b * PER_BLOCK, (b + 1) * PER_BLOCK, settle, 0)
        block_terms(
            [(part(near, 3 * b), b, "z"), (part(near, 3 * b + 1), b, "p"), (part(near, 3 * b + 2), b, "y")]
        )
        return carry

    lax.fori_loop(0, 4, near_blocks, 0)
    save = pltpu.make_async_copy(grad, grad_out.at[0], local_sem.at[1])
    save.start()

    c_copy = remote(half.at[1 - core], core_in, c_send, c_recv, partner)
    c_copy.start()
    c_copy.wait_recv()
    for q in range(4):
        for k in range(4):
            rows_k = pl.ds(q * 128 + k * 32, 32)
            x_buf[k, pl.ds(q * 32, 32), :] = half[core, rows_k, :] + core_in[rows_k, :]
    x_copies = [
        remote(x_buf.at[lax.rem(x + k, 4)], x_in.at[k - 1], xs.at[k - 1], xr.at[k - 1], x_peer(k)) for k in range(1, 4)
    ]
    for copy in x_copies:
        copy.start()
    for copy in x_copies:
        copy.wait_recv()
    for q in range(4):
        band = pl.ds(q * 32, 32)
        total = x_buf[x, band, :] + x_in[0, band, :] + x_in[1, band, :] + x_in[2, band, :]
        for k in range(8):
            y_buf[k, pl.ds(q * 4, 4), :] = total[k * 4:(k + 1) * 4, :]
    y_copies = [
        remote(y_buf.at[lax.rem(y + k, 8)], y_in.at[k - 1], ys.at[k - 1], yr.at[k - 1], y_peer(k)) for k in range(1, 8)
    ]
    for copy in y_copies:
        copy.start()
    for copy in y_copies:
        copy.wait_recv()
    total = y_buf[y]
    for k in range(7):
        total += y_in[k]
    for q in range(4):
        z_buf[q, pl.ds(0, 4), :] = total[q * 4:(q + 1) * 4, :]
        z_buf[q, pl.ds(4, 4), :] = jnp.zeros((4, 256), f32)
    z_copies = [
        remote(z_buf.at[lax.rem(z + k, 4)], z_in.at[k - 1], zs.at[k - 1], zr.at[k - 1], z_peer(k)) for k in range(1, 8)
    ]
    for copy in z_copies:
        copy.start()
    for copy in z_copies:
        copy.wait_recv()
    total = z_buf[z_low]
    for k in range(7):
        total += z_in[k]
    total = total * f32(1.0 / N)
    last_buf[...] = total
    l_copy = remote(last_buf, last_in, ls, lr, partner)
    l_copy.start()
    l_copy.wait_recv()

    @pl.when(core == 0)
    def _():
        density_out[:, 0:256] = total[0:4, :]
        density_out[:, 256:512] = last_in[0:4, :]

    @pl.when(core == 1)
    def _():
        density_out[:, 0:256] = last_in[0:4, :]
        density_out[:, 256:512] = total[0:4, :]

    o_copy.wait_send()

    def drain(p, carry):
        z_copy(p).wait_send()

        @pl.when(has_target)
        def _():
            y_copy(p).wait_send()

        @pl.when(gives_z | has_source)
        def _():
            p_copy(p, 0).wait_send()

        return carry

    lax.fori_loop(0, PIECES, drain, 0)
    for copy in [c_copy, *x_copies, *y_copies, *z_copies, l_copy]:
        copy.wait_send()
    save.wait()


def body(slabs, occ_energy, vir_energy, pair_mask):
    dma = pltpu.SemaphoreType.DMA
    vmem = pltpu.VMEM
    smem = pl.BlockSpec(memory_space=pltpu.SMEM)
    whole = pl.BlockSpec(memory_space=pltpu.VMEM)
    anywhere = pl.BlockSpec(memory_space=pl.ANY)
    return pl.pallas_call(
        kernel,
        out_shape=(jax.ShapeDtypeStruct((1, V, A), f32), jax.ShapeDtypeStruct((4, V), f32)),
        in_specs=[anywhere, smem, whole, smem],
        out_specs=(anywhere, whole),
        scratch_shapes=[
            vmem((V, A), bf16), vmem((V, A), bf16), vmem((V, A), f32), vmem((V, A), f32),
            vmem((12 * BLOCK, A), f32), vmem((V, A), f32), vmem((2, V, V // 2), f32), vmem((V, 128), f32),
            vmem((3 * BLOCK, A), bf16), vmem((3 * BLOCK, A), bf16),
            vmem((V, 3 * BLOCK), bf16), vmem((V, 3 * BLOCK), bf16),
            vmem((V, 256), f32), vmem((4, 128, 256), f32), vmem((3, 128, 256), f32),
            vmem((8, 16, 256), f32), vmem((7, 16, 256), f32), vmem((4, 8, 256), f32), vmem((7, 8, 256), f32),
            vmem((8, 256), f32), vmem((8, 256), f32),
            dma((2,)), dma, dma, dma((PIECES,)), dma((PIECES,)), dma((PIECES,)), dma((PIECES,)), dma((PIECES,)),
            dma((PIECES,)), dma, dma, dma((3,)), dma((3,)), dma((7,)), dma((7,)), dma((7,)), dma((7,)), dma, dma,
        ],
        compiler_params=pltpu.CompilerParams(
            collective_id=0, has_side_effects=True, vmem_limit_bytes=60 * 1024 * 1024
        ),
    )(slabs, occ_energy, vir_energy[None, :], pair_mask)


def solution(mesh):
    placed = (P(("occ", "grp"), None, None), P(), P(), P())
    return jax.shard_map(
        body,
        mesh=mesh,
        in_specs=placed,
        out_specs=(P(("occ", "grp"), None, None), P("occ", None)),
        check_vma=False,
    )
```

```python
import functools

import jax
import jax.numpy as jnp
from jax import lax
from jax.experimental import pallas as pl
from jax.experimental.pallas import tpu as pltpu
from jax.sharding import PartitionSpec as P

MESH = pl.DeviceIdType.MESH
V, A, N = 512, 1024, 512
BLOCK = 128
PIECE = 32
PIECES = V // PIECE
PER_BLOCK = BLOCK // PIECE
WINDOW = 8
bf16, f32 = jnp.bfloat16, jnp.float32


def device(x, y, z, core):
    return (lax.rem(z, 4) * 32 + x * 8 + y, (z // 4) * 2 + core)


def split(value):
    high = value.astype(bf16)
    return high, (value - high.astype(f32)).astype(bf16)


def times(left, right):
    return jnp.dot(left, right, preferred_element_type=f32)


def times_t(left, right):
    return lax.dot_general(left, right, (((1,), (1,)), ((), ())), preferred_element_type=f32)


def kernel(
    slab, occ_ref, vir_ref, mask_ref, grad_out, density_out,
    own_high, own_low, own, other, near, grad, half, vir_col,
    rhs_high, rhs_low, t_high, t_low,
    core_in, x_buf, x_in, y_buf, y_in, z_buf, z_in, last_buf, last_in,
    relay_buf, local_sem, o_send, o_recv, z_send, z_recv, y_send, y_recv, p_send, p_recv,
    c_send, c_recv, xs, xr, ys, yr, zs, zr, ls, lr, r_send, r_recv,
):
    occ, grp = lax.axis_index("occ"), lax.axis_index("grp")
    x, y = lax.rem(occ // 8, 4), lax.rem(occ, 8)
    z_low, z_high, core = occ // 32, grp // 2, lax.rem(grp, 2)
    z = z_high * 4 + z_low
    position = occ * 4 + grp
    partner = device(x, y, z, 1 - core)
    antipode = device(x, y, lax.rem(z + 4, 8), core)
    step = 1 - 2 * z_high
    target, source = occ + step, occ - step
    has_target = (target >= 0) & (target < 128)
    has_source = (source >= 0) & (source < 128)
    gives_z = z_high == core
    turn = jnp.where(z_high == 0, 31, 0)
    is_origin = has_target & (lax.rem(occ, 32) == turn)
    is_end = has_source & (lax.rem(source, 32) == turn)
    lane = jnp.where(z_high == 0, y, 7 - y)
    block_end = (occ // 32) * 32 + 31 - turn
    block_origin = block_end - step
    is_relay = (x == jnp.where(z_high == 0, 3, 0)) & (lane >= 1) & (block_origin >= 0) & (block_origin < 128)

    load = pltpu.make_async_copy(slab.at[0], own, local_sem.at[0])
    load.start()

    def x_peer(k):
        return device(lax.rem(x + k, 4), y, z, core)

    def y_peer(k):
        return device(x, lax.rem(y + k, 8), z, core)

    def z_peer(k):
        return device(x, y, lax.rem(z + k, 8), core)

    barrier = pltpu.get_barrier_semaphore()
    peers = [partner]
    peers += [x_peer(k) for k in range(1, 4)]
    peers += [y_peer(k) for k in range(1, 8)]
    peers += [z_peer(k) for k in range(1, 8)]
    peers += [(lax.rem(occ + k, 128), grp) for k in (1, 127)]
    for peer in peers:
        pl.semaphore_signal(barrier, inc=1, device_id=peer, device_id_type=MESH)

    @pl.when(is_end)
    def _():
        for k in range(1, 8):
            pl.semaphore_signal(barrier, inc=1, device_id=(occ + step * (24 + k), grp), device_id_type=MESH)

    @pl.when(is_relay)
    def _():
        pl.semaphore_signal(barrier, inc=1, device_id=(block_origin, grp), device_id_type=MESH)

    extra = is_relay.astype(jnp.int32) + 7 * is_origin.astype(jnp.int32)
    pl.semaphore_wait(barrier, len(peers) + extra)

    def rows(p):
        return pl.ds(pl.multiple_of(p * PIECE, PIECE), PIECE)

    def spot(kind, p):
        start = ((p // PER_BLOCK) * 3 + kind) * BLOCK + lax.rem(p, PER_BLOCK) * PIECE
        return near.at[pl.ds(pl.multiple_of(start, PIECE), PIECE)]

    def remote(src, dst, send, recv, to):
        return pltpu.make_async_remote_copy(
            src_ref=src, dst_ref=dst, send_sem=send, recv_sem=recv, device_id=to, device_id_type=MESH
        )

    def z_copy(p):
        return remote(slab.at[0, rows(p)], spot(0, p), z_send.at[p], z_recv.at[p], antipode)

    def y_copy(p):
        return remote(spot(0, p), spot(2, p), y_send.at[p], y_recv.at[p], (target, grp))

    def to_relay(p):
        return remote(
            spot(0, p), relay_buf.at[p // 8], y_send.at[p], r_recv.at[p // 8], (occ + step * (25 + lax.rem(p, 8)), grp)
        )

    def from_relay(turn_number):
        return remote(
            relay_buf.at[turn_number], spot(2, turn_number * 8 + lane), r_send.at[turn_number],
            y_recv.at[turn_number * 8 + lane], (block_end, grp),
        )

    def p_copy(p, kind):
        return remote(spot(kind, p), spot(1, p), p_send.at[p], p_recv.at[p], partner)

    o_copy = remote(slab.at[0], other, o_send, o_recv, partner)

    def start_z(p, carry):
        z_copy(p).start()
        return carry

    lax.fori_loop(0, WINDOW, start_z, 0)
    o_copy.start()

    load.wait()
    vir_row = vir_ref[...]
    vir_col[...] = jnp.transpose(jnp.broadcast_to(vir_row, (128, V)))
    for m in range(4):
        high, low = split(own[pl.ds(m * 128, 128), :])
        own_high[pl.ds(m * 128, 128), :] = high
        own_low[pl.ds(m * 128, 128), :] = low
    grad[...] = jnp.zeros_like(grad)
    half[...] = jnp.zeros_like(half)

    @pl.when(jnp.logical_not(has_source))
    def _():
        for b in range(4):
            near[pl.ds((3 * b + 2) * BLOCK, BLOCK), :] = jnp.zeros((BLOCK, A), f32)

    @pl.when(jnp.logical_not(has_source) & gives_z)
    def _():
        for b in range(4):
            near[pl.ds((3 * b + 1) * BLOCK, BLOCK), :] = jnp.zeros((BLOCK, A), f32)

    own_energy = occ_ref[position]

    def weight_of(other_index):
        low, high = jnp.minimum(position, other_index), jnp.maximum(position, other_index)
        present = (low >= 0) & (high < N)
        flag = mask_ref[jnp.maximum(low, 0), high - low - 1]
        return jnp.where(present & (flag == 1), 1.0, 0.0).astype(f32)

    def energy_of(other_index):
        return occ_ref[jnp.clip(other_index, 0, N - 1)]

    side = 1 - 2 * core
    o_index, x_index = position + side, position - side
    z_index, y_index = position + 2 * step, position - 2 * step
    facts = {
        "own": (own_energy, jnp.float32(2.0)),
        "o": (energy_of(o_index), weight_of(o_index)),
        "z": (energy_of(z_index), weight_of(z_index)),
        "p": (energy_of(x_index), weight_of(x_index)),
        "y": (energy_of(y_index), weight_of(y_index)),
    }

    def tiles_of(pieces):
        tiles = []
        for _, number, name in pieces:
            energy, weight = facts[name]
            start = pl.multiple_of(number * BLOCK, BLOCK)
            tiles.append((own_energy + energy - vir_ref[:, pl.ds(start, BLOCK)], weight))
        return tiles

    def weighted(ref, slot, band, names):
        parts = [
            ref[slot, band, n * BLOCK:(n + 1) * BLOCK] * facts[name][1].astype(bf16) for n, name in enumerate(names)
        ]
        return parts[0] if len(parts) == 1 else jnp.concatenate(parts, axis=1)

    def amplitudes(slot, pieces):
        width = len(pieces) * BLOCK
        names = [name for _, _, name in pieces]
        for n, (ref, _, _) in enumerate(pieces):
            high, low = split(ref[...])
            rhs_high[slot, pl.ds(n * BLOCK, BLOCK), :] = high
            rhs_low[slot, pl.ds(n * BLOCK, BLOCK), :] = low
        tiles = tiles_of(pieces)

        def rows_of(m, carry):
            band = pl.ds(pl.multiple_of(m * 256, 256), 256)
            left_high, left_low = own_high[band, :], own_low[band, :]
            right_high, right_low = rhs_high[slot, :width, :], rhs_low[slot, :width, :]
            coulomb = times_t(left_high, right_high)
            coulomb += times_t(left_high, right_low)
            coulomb += times_t(left_low, right_high)
            column = vir_col[band, :]
            for n, (base, _) in enumerate(tiles):
                cut = slice(n * BLOCK, (n + 1) * BLOCK)
                high, low = split(coulomb[:, cut] / (base - column))
                t_high[slot, band, cut] = high
                t_low[slot, band, cut] = low
            return carry

        lax.fori_loop(0, 2, rows_of, 0)

        def density_rows(m, carry):
            band = pl.ds(pl.multiple_of(m * 256, 256), 256)
            left_high, left_low = weighted(t_high, slot, band, names), weighted(t_low, slot, band, names)
            for h in range(2):
                other_high = t_high[slot, pl.ds(h * 256, 256), :width]
                other_low = t_low[slot, pl.ds(h * 256, 256), :width]
                half[h, band, :] += (
                    times_t(left_high, other_high) + times_t(left_high, other_low) + times_t(left_low, other_high)
                )
            return carry

        lax.fori_loop(0, 2, density_rows, 0)

    def gradient(slot, names):
        width = len(names) * BLOCK

        def rows_of(m, carry):
            band = pl.ds(pl.multiple_of(m * 256, 256), 256)
            left_high, left_low = weighted(t_high, slot, band, names), weighted(t_low, slot, band, names)
            right_high, right_low = rhs_high[slot, :width, :], rhs_low[slot, :width, :]
            grad[band, :] += times(left_high, right_high) + times(left_high, right_low) + times(left_low, right_high)
            return carry

        lax.fori_loop(0, 2, rows_of, 0)

    def part(ref, b):
        return ref.at[pl.ds(pl.multiple_of(b * BLOCK, BLOCK), BLOCK)]

    def own_blocks(b, carry):
        amplitudes(4, [(part(own, 2 * b), 2 * b, "own"), (part(own, 2 * b + 1), 2 * b + 1, "own")])
        gradient(4, ["own", "own"])
        return carry

    lax.fori_loop(0, 2, own_blocks, 0)
    o_copy.wait_recv()

    def other_blocks(b, carry):
        amplitudes(4, [(part(other, 2 * b), 2 * b, "o"), (part(other, 2 * b + 1), 2 * b + 1, "o")])
        gradient(4, ["o", "o"])
        return carry

    lax.fori_loop(0, 2, other_blocks, 0)

    def take(p, carry):
        z_copy(p).wait_recv()

        relayed = is_origin & (lax.rem(p, 8) != 0)

        @pl.when(has_target & jnp.logical_not(relayed))
        def _():
            y_copy(p).start()

        @pl.when(relayed)
        def _():
            to_relay(p).start()

        @pl.when(gives_z)
        def _():
            p_copy(p, 0).start()

        @pl.when(p + WINDOW < PIECES)
        def _():
            z_copy(p).wait_send()
            z_copy(p + WINDOW).start()

        return carry

    def pass_on(p, carry):
        @pl.when(has_source)
        def _():
            y_copy(p).wait_recv()

            @pl.when(jnp.logical_not(gives_z))
            def _():
                p_copy(p, 2).start()

        return carry

    def over(b, step_of):
        lax.fori_loop(b * PER_BLOCK, (b + 1) * PER_BLOCK, step_of, 0)

    def settle(p, carry):
        @pl.when(has_source | jnp.logical_not(gives_z))
        def _():
            p_copy(p, 0).wait_recv()

        return carry

    over(0, take)

    def hand_on(h):
        to_relay(h * 8).wait_recv()
        from_relay(h).start()

    def near_blocks(b, carry):
        amplitudes(4, [(part(near, 3 * b), b, "z")])
        gradient(4, ["z"])

        @pl.when(is_relay & (lane < 4) & (b == 2))
        def _():
            hand_on(1)

        @pl.when(b < 3)
        def _():
            over(b + 1, take)

        @pl.when(is_relay & (((b == 0) & (lane < 4)) | ((b == 1) & (lane >= 4))))
        def _():
            hand_on(0)

        @pl.when(is_relay & (lane >= 4) & (b == 2))
        def _():
            hand_on(1)

        over(b, pass_on)
        over(b, settle)
        amplitudes(b, [(part(near, 3 * b + 1), b, "p"), (part(near, 3 * b + 2), b, "y")])
        return carry

    lax.fori_loop(0, 4, near_blocks, 0)

    c_copy = remote(half.at[1 - core], core_in, c_send, c_recv, partner)
    c_copy.start()
    gradient(0, ["p", "y"])
    c_copy.wait_recv()
    for q in range(4):
        for k in range(4):
            rows_k = pl.ds(q * 128 + k * 32, 32)
            x_buf[k, pl.ds(q * 32, 32), :] = half[core, rows_k, :] + core_in[rows_k, :]
    x_copies = [
        remote(x_buf.at[lax.rem(x + k, 4)], x_in.at[k - 1], xs.at[k - 1], xr.at[k - 1], x_peer(k)) for k in range(1, 4)
    ]
    for copy in x_copies:
        copy.start()
    gradient(1, ["p", "y"])
    gradient(2, ["p", "y"])
    for copy in x_copies:
        copy.wait_recv()
    for q in range(4):
        band = pl.ds(q * 32, 32)
        total = x_buf[x, band, :] + x_in[0, band, :] + x_in[1, band, :] + x_in[2, band, :]
        for k in range(8):
            y_buf[k, pl.ds(q * 4, 4), :] = total[k * 4:(k + 1) * 4, :]
    y_copies = [
        remote(y_buf.at[lax.rem(y + k, 8)], y_in.at[k - 1], ys.at[k - 1], yr.at[k - 1], y_peer(k)) for k in range(1, 8)
    ]
    for copy in y_copies:
        copy.start()
    gradient(3, ["p", "y"])
    save = pltpu.make_async_copy(grad, grad_out.at[0], local_sem.at[1])
    save.start()
    for copy in y_copies:
        copy.wait_recv()
    total = y_buf[y]
    for k in range(7):
        total += y_in[k]
    for q in range(4):
        z_buf[q, pl.ds(0, 4), :] = total[q * 4:(q + 1) * 4, :]
        z_buf[q, pl.ds(4, 4), :] = jnp.zeros((4, 256), f32)
    z_copies = [
        remote(z_buf.at[lax.rem(z + k, 4)], z_in.at[k - 1], zs.at[k - 1], zr.at[k - 1], z_peer(k)) for k in range(1, 8)
    ]
    for copy in z_copies:
        copy.start()
    for copy in z_copies:
        copy.wait_recv()
    total = z_buf[z_low]
    for k in range(7):
        total += z_in[k]
    total = total * f32(1.0 / N)
    last_buf[...] = total
    l_copy = remote(last_buf, last_in, ls, lr, partner)
    l_copy.start()
    l_copy.wait_recv()

    @pl.when(core == 0)
    def _():
        density_out[:, 0:256] = total[0:4, :]
        density_out[:, 256:512] = last_in[0:4, :]

    @pl.when(core == 1)
    def _():
        density_out[:, 0:256] = last_in[0:4, :]
        density_out[:, 256:512] = total[0:4, :]

    o_copy.wait_send()

    @pl.when(is_relay)
    def _():
        for h in range(2):
            from_relay(h).wait_send()

    def drain(p, carry):
        @pl.when(p + WINDOW >= PIECES)
        def _():
            z_copy(p).wait_send()

        @pl.when(has_target)
        def _():
            y_copy(p).wait_send()

        @pl.when(gives_z | has_source)
        def _():
            p_copy(p, 0).wait_send()

        return carry

    lax.fori_loop(0, PIECES, drain, 0)
    for copy in [c_copy, *x_copies, *y_copies, *z_copies, l_copy]:
        copy.wait_send()
    save.wait()


def body(slabs, occ_energy, vir_energy, pair_mask):
    dma = pltpu.SemaphoreType.DMA
    vmem = pltpu.VMEM
    smem = pl.BlockSpec(memory_space=pltpu.SMEM)
    whole = pl.BlockSpec(memory_space=pltpu.VMEM)
    anywhere = pl.BlockSpec(memory_space=pl.ANY)
    return pl.pallas_call(
        kernel,
        out_shape=(jax.ShapeDtypeStruct((1, V, A), f32), jax.ShapeDtypeStruct((4, V), f32)),
        in_specs=[anywhere, smem, whole, smem],
        out_specs=(anywhere, whole),
        scratch_shapes=[
            vmem((V, A), bf16), vmem((V, A), bf16), vmem((V, A), f32), vmem((V, A), f32),
            vmem((12 * BLOCK, A), f32), vmem((V, A), f32), vmem((2, V, V // 2), f32), vmem((V, 128), f32),
            vmem((5, 2 * BLOCK, A), bf16), vmem((5, 2 * BLOCK, A), bf16),
            vmem((5, V, 2 * BLOCK), bf16), vmem((5, V, 2 * BLOCK), bf16),
            vmem((V, 256), f32), vmem((4, 128, 256), f32), vmem((3, 128, 256), f32),
            vmem((8, 16, 256), f32), vmem((7, 16, 256), f32), vmem((4, 8, 256), f32), vmem((7, 8, 256), f32),
            vmem((8, 256), f32), vmem((8, 256), f32), vmem((2, PIECE, A), f32),
            dma((2,)), dma, dma, dma((PIECES,)), dma((PIECES,)), dma((PIECES,)), dma((PIECES,)), dma((PIECES,)),
            dma((PIECES,)), dma, dma, dma((3,)), dma((3,)), dma((7,)), dma((7,)), dma((7,)), dma((7,)), dma, dma,
            dma((2,)), dma((2,)),
        ],
        compiler_params=pltpu.CompilerParams(
            collective_id=0, has_side_effects=True, vmem_limit_bytes=34 * 1024 * 1024
        ),
    )(slabs, occ_energy, vir_energy[None, :], pair_mask)


def solution(mesh):
    placed = (P(("occ", "grp"), None, None), P(), P(), P())
    return jax.shard_map(
        body,
        mesh=mesh,
        in_specs=placed,
        out_specs=(P(("occ", "grp"), None, None), P("occ", None)),
        check_vma=False,
    )
```
